32 devices in a mesh: row: 8 (over y, x, core), blk: 4 (over z).
Axes of the slice: x: 2, y: 2, z: 4, core: 2. Of those that a mesh axis runs over, the one named last changes fastest.
Arguments:
- values: bfloat16 [512, 16, 256, 256], P('row', 'blk'), may hold values from -6 to 6
- scales: bfloat16 [512, 16], P('row', 'blk'), may hold values from 0.0049743652 to 0.049804688
- pattern: int32 [512, 16], P('row', 'blk'), may hold values from 0 to 2047, as said below
- omega: bfloat16 [2048, 256, 128], P(('row', 'blk')), may hold values from -6 to 6
Outputs:
- basis: float32 [2048, 256, 128], P(('row', 'blk'))
- upper: float32 [128, 128], replicated
The draws below stay inside these ranges and needn't reach their ends.
Inputs may be any that keep to these rules, and one draw needn't show every extreme that they name: `pattern`: A block-row of group g = r // 64 has all its column blocks in g * 256 to (g + 1) * 256 - 1. Among the 256 blocks of one device (its block-rows and its positions), at most 64 lie in one aligned run of 64 column blocks, and some run holds exactly 64.
All inputs are finite; a program needn't handle non-finite values.
Results may differ from the reference program's by a relative error of at most 0.0003.
Values may be sent and summed in bfloat16 or wider, within the bound.
A program may use at most 192 MiB of HBM per device.

```python
import math
import jax
import jax.numpy as jnp
from jax import lax

BS = 256
P_SIZE = 128
NCB = 2048
K = 16
RB = 64
KDEV = 4
MB = 512
CAP = 64


def draw_pattern(key, part):
    block_count = RB * KDEV
    cycle_size = K // KDEV
    row_groups = MB // RB
    col_per_dev = NCB // (row_groups * cycle_size)

    def one_device(index):
        device_key = jax.random.fold_in(key, index)
        key_hot, key_perm, key_local = jax.random.split(device_key, 3)
        hot_owner = jax.random.randint(key_hot, (), 0, cycle_size)
        slots = jnp.arange(block_count)
        others = (hot_owner + 1 + (slots - CAP) % (cycle_size - 1)) % cycle_size
        owner_list = jnp.where(slots < CAP, hot_owner, others)
        owner_list = jax.random.permutation(key_perm, owner_list)
        local_list = jax.random.randint(key_local, (block_count,), 0, col_per_dev)
        group_base = index // cycle_size * col_per_dev * cycle_size
        return (group_base + owner_list * col_per_dev + local_list).reshape(RB, KDEV)
    tables = jax.vmap(one_device)(jnp.arange(row_groups * cycle_size))
    return tables.reshape(row_groups, cycle_size, RB, KDEV).transpose(0, 2, 1, 3).reshape(MB, K).astype(jnp.int32)


def levels(own_key, shape, cuts, smallest, largest):
    def one(dim, parts):
        steps = jax.random.uniform(jax.random.fold_in(jax.random.fold_in(own_key, 6), dim), (parts,), jnp.float32, smallest / len(cuts), largest / len(cuts))
        return jnp.repeat(jnp.exp(steps), shape[dim] // parts).reshape((-1,) + (1,) * (len(shape) - dim - 1))

    gain = one(*cuts[0])
    for cut in cuts[1:]:
        gain = gain * one(*cut)
    return gain


def normal_values(stream_key, shape, width, reach, pieces=(), dtype=jnp.bfloat16):
    result = width * jax.random.normal(stream_key, shape, jnp.float32)
    if pieces:
        result = result * levels(stream_key, shape, pieces, -0.22, 0.18)
    return jnp.clip(result, -reach, reach).astype(dtype)


def setup_inputs(seed: int = 0) -> dict:
    key_of = jax.random.split(jax.random.key(seed), 5)
    return {
        "values": normal_values(key_of[0], (MB, K, BS, BS), 1.0, 6.0, ((0, 8), (1, 4))),
        "scales": jnp.clip(jnp.exp(math.log(0.049804688) - 2.3038113 * jax.random.uniform(key_of[1], (MB, K), jnp.float32) ** levels(key_of[1], (MB, K), ((0, 8), (1, 4)), -0.2, 0.2)), 0.0049743652, 0.049804688).astype(jnp.bfloat16),
        "pattern": draw_pattern(jax.random.fold_in(key_of[4], 71), 0),
        "omega": normal_values(key_of[3], (NCB, BS, P_SIZE), 1.0, 6.0, ((0, 32),)),
    }


def reference(values, scales, pattern, omega):
    weights = scales.astype(jnp.float32)

    def row_product(item_tuple):
        blocks, scale_row, col_blocks = item_tuple
        picked = jnp.take(omega, col_blocks, axis=0).astype(jnp.float32)
        products = jnp.einsum('kij,kjc->kic', blocks.astype(jnp.float32), picked) * scale_row[:, None, None]
        partial_value = jnp.sum(products.reshape(K // KDEV, KDEV, BS, P_SIZE), axis=1)
        return jnp.sum(partial_value, axis=0)
    rowvec = lax.map(row_product, (values, weights, pattern))

    def add_row(running_sum, item_tuple):
        blocks, scale_row, col_blocks, row_vecs = item_tuple
        row_high = lax.optimization_barrier(row_vecs.astype(jnp.bfloat16))
        row_low = (row_vecs - row_high.astype(jnp.float32)).astype(jnp.bfloat16)
        blocks_wide = blocks.astype(jnp.float32)
        high_part = jnp.einsum('kji,jc->kic', blocks_wide, row_high.astype(jnp.float32))
        low_part = jnp.einsum('kji,jc->kic', blocks_wide, row_low.astype(jnp.float32))
        contrib = (high_part + low_part) * scale_row[:, None, None]
        return (running_sum.at[col_blocks].add(contrib), None)
    start_sum = jnp.zeros((NCB, BS, P_SIZE), jnp.float32)
    colsum, unused = lax.scan(add_row, start_sum, (values, weights, pattern, rowvec))
    flat_sum = colsum.reshape(NCB * BS, P_SIZE)
    gram = jnp.dot(flat_sum.T, flat_sum, precision=lax.Precision.HIGHEST) / (NCB * BS)
    lower_factor = jnp.linalg.cholesky(gram)
    solved = jax.scipy.linalg.solve_triangular(lower_factor, flat_sum.T, lower=True)
    return (solved.T.reshape(NCB, BS, P_SIZE), lower_factor.T)
```

```python
import jax
import jax.numpy as jnp
from jax import lax
from jax.experimental import pallas as pl
from jax.experimental.pallas import tpu as pltpu
from jax.sharding import PartitionSpec as P

LEVELS = 32767.0


def encode(x):
    peak = jnp.max(jnp.abs(x), axis=1)
    inverse = jnp.where(peak > 0, LEVELS / jnp.where(peak > 0, peak, 1.0), 0.0)
    code = jnp.clip(jnp.round(x * inverse[:, None, :]), -LEVELS, LEVELS)
    return code.astype(jnp.int32).astype(jnp.int16), peak * (1.0 / LEVELS)


def decode(code, step):
    return code.astype(jnp.int32).astype(jnp.float32) * step[:, None, :]


def send(coded, pairs):
    return tuple(lax.ppermute(part, "blk", pairs) for part in coded)


def line_reduce(first, own, n, me):
    start = encode(first)
    right = left = None
    for t in range(n - 1):
        if t == 0:
            to_right = to_left = start
        else:
            to_right = encode(own(jnp.minimum(me + n - 1 - t, n - 1)) + decode(*right))
            to_left = encode(own(jnp.maximum(me - (n - 1) + t, 0)) + decode(*left))
        right = send(to_right, [(i, i + 1) for i in range(t + 1)])
        left = send(to_left, [(i, i - 1) for i in range(n - 1 - t, n)])
    return own(me) + decode(*right) + decode(*left)


def all_sum(x, axis):
    n = lax.axis_size(axis)
    if n & (n - 1):
        return lax.psum(x, axis)
    bit = 1
    while bit < n:
        x = x + lax.ppermute(x, axis, [(i, i ^ bit) for i in range(n)])
        bit *= 2
    return x


def forward(values, weights, cols, slab):
    rows, per, side, _ = values.shape
    count, _, width = slab.shape
    batch = 4 if rows % 4 == 0 else 1

    def body(cols_ref, weights_ref, values_ref, slab_ref, out_ref):
        base = pl.program_id(0) * (batch * per)
        for r in range(batch):
            total = None
            for k in range(per):
                at = base + r * per + k
                term = weights_ref[at] * jnp.dot(
                    values_ref[r, k], slab_ref[cols_ref[at]], preferred_element_type=jnp.float32
                )
                total = term if total is None else total + term
            out_ref[r] = total

    return pl.pallas_call(
        body,
        out_shape=jax.ShapeDtypeStruct((rows, side, width), jnp.float32),
        grid_spec=pltpu.PrefetchScalarGridSpec(
            num_scalar_prefetch=2,
            grid=(rows // batch,),
            in_specs=[
                pl.BlockSpec((batch, per, side, side), lambda i, *_: (i, 0, 0, 0)),
                pl.BlockSpec(
                    (count, side, width), lambda i, *_: (0, 0, 0), pipeline_mode=pl.Buffered(1)
                ),
            ],
            out_specs=pl.BlockSpec((batch, side, width), lambda i, *_: (i, 0, 0)),
        ),
        compiler_params=pltpu.CompilerParams(vmem_limit_bytes=48 << 20),
        cost_estimate=pl.CostEstimate(
            flops=2 * rows * per * side * side * width,
            bytes_accessed=2 * values.size + 2 * slab.size + 4 * rows * side * width,
            transcendentals=0,
        ),
        name="forward",
    )(cols, weights, values, slab)


def backward(blocks, weights, local_cols, order, dests, both, n, per, col_dev):
    total, side, _ = blocks.shape
    rows, _, twice = both.shape
    width = twice // 2
    cap = total // n
    batch = 4 if cap % 4 == 0 else 1
    groups = dests.shape[0]

    def body(order_ref, dest_ref, cols_ref, weights_ref, *refs):
        block_refs, both_ref, out_ref = refs[:batch], refs[batch], refs[batch + 1]

        @pl.when(pl.program_id(1) == 0)
        def _():
            out_ref[...] = jnp.zeros_like(out_ref)

        base = dest_ref[pl.program_id(0)] * cap + pl.program_id(1) * batch
        for u in range(batch):
            at = order_ref[base + u]
            pair = lax.dot_general(
                block_refs[u][0],
                both_ref[at // per],
                (((0,), (0,)), ((), ())),
                preferred_element_type=jnp.float32,
            )
            term = weights_ref[at] * (pair[:, :width] + pair[:, width:])
            out_ref[0, cols_ref[at]] += term

    def block_spec(u):
        return pl.BlockSpec(
            (1, side, side),
            lambda g, i, order, dest, *_: (order[dest[g] * cap + i * batch + u], 0, 0),
        )

    return pl.pallas_call(
        body,
        out_shape=jax.ShapeDtypeStruct((groups, col_dev, side, width), jnp.float32),
        grid_spec=pltpu.PrefetchScalarGridSpec(
            num_scalar_prefetch=4,
            grid=(groups, cap // batch),
            in_specs=[block_spec(u) for u in range(batch)]
            + [
                pl.BlockSpec(
                    (rows, side, twice), lambda g, i, *_: (0, 0, 0), pipeline_mode=pl.Buffered(1)
                )
            ],
            out_specs=pl.BlockSpec((1, col_dev, side, width), lambda g, i, *_: (g, 0, 0, 0)),
        ),
        compiler_params=pltpu.CompilerParams(vmem_limit_bytes=48 << 20),
        cost_estimate=pl.CostEstimate(
            flops=2 * groups * cap * side * side * twice,
            bytes_accessed=2 * groups * cap * side * side
            + 2 * both.size
            + 4 * groups * col_dev * side * width,
            transcendentals=0,
        ),
        name="backward",
    )(order, dests, local_cols, weights, *([blocks] * batch), both)


def local(values, scales, pattern, omega):
    rows, per = pattern.shape
    col_dev, side, width = omega.shape
    n = lax.axis_size("blk")
    me = lax.axis_index("blk")
    count = rows * per
    cols = pattern.reshape(-1) - lax.axis_index("row") * (col_dev * n)
    weights = scales.astype(jnp.float32).reshape(-1)
    slot = jnp.arange(count)
    before = (cols[None, :] < cols[:, None]) | (
        (cols[None, :] == cols[:, None]) & (slot[None, :] < slot[:, None])
    )
    rank = jnp.sum(before.astype(jnp.int32), axis=1)
    order = jnp.sum(jnp.where(rank[None, :] == slot[:, None], slot[None, :], 0), axis=1)
    local_cols = cols % col_dev

    slab = lax.all_gather(omega, "blk", axis=0, tiled=True)
    partial = forward(values, weights, cols, slab)

    share = rows // n
    edge = jnp.where(me < n // 2, n - 1, 0)

    def rows_of(d):
        return lax.dynamic_slice_in_dim(partial, d * share, share, axis=0)

    code, step = encode(line_reduce(rows_of(edge), rows_of, n, me))
    code = lax.all_gather(code, "blk", axis=0, tiled=True)
    step = lax.all_gather(step, "blk", axis=0, tiled=True)
    row_total = decode(code, step)
    high = lax.optimization_barrier(row_total.astype(jnp.bfloat16))
    low = (row_total - high.astype(jnp.float32)).astype(jnp.bfloat16)
    both = jnp.concatenate([high, low], axis=2)

    blocks = values.reshape(count, side, side)
    first = backward(
        blocks, weights, local_cols, order, edge.reshape(1).astype(jnp.int32), both, n, per, col_dev
    )
    every = backward(
        blocks, weights, local_cols, order, jnp.arange(n, dtype=jnp.int32), both, n, per, col_dev
    )

    parts = 2 if col_dev % 2 == 0 else 1
    piece = col_dev // parts
    sums = []
    for p in range(parts):

        def own(d, p=p):
            return lax.dynamic_slice(
                every, (d, p * piece, 0, 0), (1, piece, side, width)
            )[0]

        sums.append(line_reduce(first[0, p * piece : (p + 1) * piece], own, n, me))
    flat_sum = jnp.concatenate(sums, axis=0).reshape(col_dev * side, width)

    gram_local = jnp.dot(flat_sum.T, flat_sum, precision=lax.Precision.HIGHEST)
    total_rows = col_dev * side * n * lax.axis_size("row")
    gram = all_sum(all_sum(gram_local, "row"), "blk") / total_rows
    lower_factor = jnp.linalg.cholesky(gram)
    solved = jax.scipy.linalg.solve_triangular(lower_factor, flat_sum.T, lower=True)
    return (solved.T.reshape(col_dev, side, width), lower_factor.T)


def solution(mesh):
    return jax.shard_map(
        local,
        mesh=mesh,
        in_specs=(
            P("row", "blk", None, None),
            P("row", "blk"),
            P("row", "blk"),
            P(("row", "blk"), None, None),
        ),
        out_specs=(P(("row", "blk"), None, None), P()),
        check_vma=False,
    )
```

```python
import jax
import jax.numpy as jnp
from jax import lax
from jax.experimental import pallas as pl
from jax.experimental.pallas import tpu as pltpu
from jax.sharding import PartitionSpec as P

LEVELS = 32767.0


def encode(x):
    peak = jnp.max(jnp.abs(x), axis=1)
    inverse = jnp.where(peak > 0, LEVELS / jnp.where(peak > 0, peak, 1.0), 0.0)
    code = jnp.clip(jnp.round(x * inverse[:, None, :]), -LEVELS, LEVELS)
    return code.astype(jnp.int32).astype(jnp.int16), peak * (1.0 / LEVELS)


def decode(code, step):
    return code.astype(jnp.int32).astype(jnp.float32) * step[:, None, :]


def send(coded, pairs):
    return tuple(lax.ppermute(part, "blk", pairs) for part in coded)


def line_reduce(first, own, n, me):
    start = encode(first)
    right = left = None
    for t in range(n - 1):
        if t == 0:
            to_right = to_left = start
        else:
            to_right = encode(own(jnp.minimum(me + n - 1 - t, n - 1)) + decode(*right))
            to_left = encode(own(jnp.maximum(me - (n - 1) + t, 0)) + decode(*left))
        right = send(to_right, [(i, i + 1) for i in range(t + 1)])
        left = send(to_left, [(i, i - 1) for i in range(n - 1 - t, n)])
    return own(me) + decode(*right) + decode(*left)


def line_gather(parts, n, me):
    right = left = parts
    whole = []
    for part in parts:
        empty = jnp.zeros(((n + 1) * part.shape[0],) + part.shape[1:], part.dtype)
        whole.append(lax.dynamic_update_slice_in_dim(empty, part, me * part.shape[0], axis=0))
    for t in range(n - 1):
        right = send(right, [(i, i + 1) for i in range(t, n - 1)])
        left = send(left, [(i, i - 1) for i in range(1, n - t)])
        for got, owner in ((right, me - t - 1), (left, me + t + 1)):
            at = jnp.where((owner >= 0) & (owner < n), owner, n)
            whole = [
                lax.dynamic_update_slice_in_dim(w, g, at * g.shape[0], axis=0)
                for w, g in zip(whole, got)
            ]
    return whole


def all_sum(x, axis):
    n = lax.axis_size(axis)
    if n & (n - 1):
        return lax.psum(x, axis)
    bit = 1
    while bit < n:
        x = x + lax.ppermute(x, axis, [(i, i ^ bit) for i in range(n)])
        bit *= 2
    return x


def forward(values, weights, cols, slab, count):
    rows, per, side, _ = values.shape
    width = slab.shape[2]
    batch = 4 if rows % 4 == 0 else 1

    def body(cols_ref, weights_ref, values_ref, slab_ref, out_ref):
        base = pl.program_id(0) * (batch * per)
        for r in range(batch):
            total = None
            for k in range(per):
                at = base + r * per + k
                term = weights_ref[at] * jnp.dot(
                    values_ref[r, k], slab_ref[cols_ref[at]], preferred_element_type=jnp.float32
                )
                total = term if total is None else total + term
            out_ref[r] = total

    return pl.pallas_call(
        body,
        out_shape=jax.ShapeDtypeStruct((rows, side, width), jnp.float32),
        grid_spec=pltpu.PrefetchScalarGridSpec(
            num_scalar_prefetch=2,
            grid=(rows // batch,),
            in_specs=[
                pl.BlockSpec((batch, per, side, side), lambda i, *_: (i, 0, 0, 0)),
                pl.BlockSpec(
                    (count, side, width), lambda i, *_: (0, 0, 0), pipeline_mode=pl.Buffered(1)
                ),
            ],
            out_specs=pl.BlockSpec((batch, side, width), lambda i, *_: (i, 0, 0)),
        ),
        compiler_params=pltpu.CompilerParams(vmem_limit_bytes=48 << 20),
        cost_estimate=pl.CostEstimate(
            flops=2 * rows * per * side * side * width,
            bytes_accessed=2 * values.size + 2 * count * side * width + 4 * rows * side * width,
            transcendentals=0,
        ),
        name="forward",
    )(cols, weights, values, slab)


def backward(blocks, weights, local_cols, order, dests, high, low, n, per, col_dev):
    total, side, _ = blocks.shape
    rows, _, width = high.shape
    twice = 2 * width
    cap = total // n
    batch = 4 if cap % 4 == 0 else 1
    groups = dests.shape[0]

    def body(order_ref, dest_ref, cols_ref, weights_ref, *refs):
        block_refs = refs[:batch]
        high_ref, low_ref, out_ref = refs[batch:]

        @pl.when(pl.program_id(1) == 0)
        def _():
            out_ref[...] = jnp.zeros_like(out_ref)

        base = dest_ref[pl.program_id(0)] * cap + pl.program_id(1) * batch
        for u in range(batch):
            at = order_ref[base + u]
            pair = lax.dot_general(
                block_refs[u][0],
                jnp.concatenate([high_ref[at // per], low_ref[at // per]], axis=1),
                (((0,), (0,)), ((), ())),
                preferred_element_type=jnp.float32,
            )
            term = weights_ref[at] * (pair[:, :width] + pair[:, width:])
            out_ref[0, cols_ref[at]] += term

    def block_spec(u):
        return pl.BlockSpec(
            (1, side, side),
            lambda g, i, order, dest, *_: (order[dest[g] * cap + i * batch + u], 0, 0),
        )

    return pl.pallas_call(
        body,
        out_shape=jax.ShapeDtypeStruct((groups, col_dev, side, width), jnp.float32),
        grid_spec=pltpu.PrefetchScalarGridSpec(
            num_scalar_prefetch=4,
            grid=(groups, cap // batch),
            in_specs=[block_spec(u) for u in range(batch)]
            + [
                pl.BlockSpec(
                    (rows, side, width), lambda g, i, *_: (0, 0, 0), pipeline_mode=pl.Buffered(1)
                )
            ]
            * 2,
            out_specs=pl.BlockSpec((1, col_dev, side, width), lambda g, i, *_: (g, 0, 0, 0)),
        ),
        compiler_params=pltpu.CompilerParams(vmem_limit_bytes=48 << 20),
        cost_estimate=pl.CostEstimate(
            flops=2 * groups * cap * side * side * twice,
            bytes_accessed=2 * groups * cap * side * side
            + 4 * high.size
            + 4 * groups * col_dev * side * width,
            transcendentals=0,
        ),
        name="backward",
    )(order, dests, local_cols, weights, *([blocks] * batch), high, low)


def local(values, scales, pattern, omega):
    rows, per = pattern.shape
    col_dev, side, width = omega.shape
    n = lax.axis_size("blk")
    me = lax.axis_index("blk")
    count = rows * per
    cols = pattern.reshape(-1) - lax.axis_index("row") * (col_dev * n)
    weights = scales.astype(jnp.float32).reshape(-1)
    slot = jnp.arange(count)
    before = (cols[None, :] < cols[:, None]) | (
        (cols[None, :] == cols[:, None]) & (slot[None, :] < slot[:, None])
    )
    rank = jnp.sum(before.astype(jnp.int32), axis=1)
    order = jnp.sum(jnp.where(rank[None, :] == slot[:, None], slot[None, :], 0), axis=1)
    local_cols = cols % col_dev

    (slab,) = line_gather((omega,), n, me)
    partial = forward(values, weights, cols, slab, col_dev * n)

    share = rows // n
    edge = jnp.where(me < n // 2, n - 1, 0)

    def rows_of(d):
        return lax.dynamic_slice_in_dim(partial, d * share, share, axis=0)

    code, step = encode(line_reduce(rows_of(edge), rows_of, n, me))
    code, step = line_gather((code, step), n, me)
    row_total = decode(code[:rows], step[:rows])
    high = lax.optimization_barrier(row_total.astype(jnp.bfloat16))
    low = (row_total - high.astype(jnp.float32)).astype(jnp.bfloat16)

    blocks = values.reshape(count, side, side)
    first = backward(
        blocks, weights, local_cols, order, edge.reshape(1).astype(jnp.int32), high, low, n, per, col_dev
    )
    every = backward(
        blocks, weights, local_cols, order, jnp.arange(n, dtype=jnp.int32), high, low, n, per, col_dev
    )

    parts = 2 if col_dev % 2 == 0 else 1
    piece = col_dev // parts
    sums = []
    for p in range(parts):

        def own(d, p=p):
            return lax.dynamic_slice(
                every, (d, p * piece, 0, 0), (1, piece, side, width)
            )[0]

        sums.append(line_reduce(first[0, p * piece : (p + 1) * piece], own, n, me))
    flat_sum = jnp.concatenate(sums, axis=0).reshape(col_dev * side, width)

    gram_local = jnp.dot(flat_sum.T, flat_sum, precision=lax.Precision.HIGHEST)
    total_rows = col_dev * side * n * lax.axis_size("row")
    gram = all_sum(all_sum(gram_local, "row"), "blk") / total_rows
    lower_factor = jnp.linalg.cholesky(gram)
    solved = jax.scipy.linalg.solve_triangular(lower_factor, flat_sum.T, lower=True)
    return (solved.T.reshape(col_dev, side, width), lower_factor.T)


def solution(mesh):
    return jax.shard_map(
        local,
        mesh=mesh,
        in_specs=(
            P("row", "blk", None, None),
            P("row", "blk"),
            P("row", "blk"),
            P(("row", "blk"), None, None),
        ),
        out_specs=(P(("row", "blk"), None, None), P()),
        check_vma=False,
    )
```
